32 devices in a mesh: seq: 8 (over z, x), head: 4 (over y, core).
Axes of the slice: x: 2, y: 2, z: 4, core: 2. Of those that a mesh axis runs over, the one named last changes fastest.
Arguments:
- queries: bfloat16 [6144, 8192], P('seq', 'head'), may hold values from -6 to 6
- key_rows: bfloat16 [6144, 8192], P('seq', 'head'), may hold values from -0.5 to 0.5
- value_rows: bfloat16 [6144, 8192], P('seq', 'head'), may hold values from -130 to 130
- log_decay: float32 [64, 6144], P('head', 'seq'), may hold values from -1 to 0
- norm_gain: float32 [8192], P('head'), may hold values from 0.1 to 1.9
- grad_out: bfloat16 [6144, 8192], P('seq', 'head'), may hold values from -13 to 13
Outputs:
- output: bfloat16 [6144, 8192], P('seq', 'head')
- grad_queries: bfloat16 [6144, 8192], P('seq', 'head')
- grad_keys: bfloat16 [6144, 8192], P('seq', 'head')
- grad_values: bfloat16 [6144, 8192], P('seq', 'head')
- grad_gain: float32 [8192], P('head')
The draws below stay inside these ranges and needn't reach their ends.
All inputs are finite; a program needn't handle non-finite values.
Results may differ from the reference program's by a relative error of at most 0.01.
Values sent between devices are 32-bit elements; how exact they have to be, the bound alone decides.
A program may use at most 192 MiB of HBM per device.

```python
import jax
import jax.numpy as jnp
from jax import lax

HEADS = 64
DH = 128
TOK_DEV = 768
SEQUENCE_TOKENS = 6144
HD = 8192


def draw_log_decay(key, part):
    sample_sequences = jax.random.split(key, 6)
    token_position = jnp.arange(SEQUENCE_TOKENS)
    fast_share = 0.5
    picked = jax.random.uniform(sample_sequences[0], (HEADS, 1), dtype=jnp.float32)
    fast_rate = jnp.exp(jax.random.uniform(sample_sequences[1], (HEADS, 1), dtype=jnp.float32, minval=jnp.log(1.0 / 50.0), maxval=jnp.log(1.0 / 30.0)))
    slow_rate = 0.6 / SEQUENCE_TOKENS
    baseline_decay_rate = jnp.where(picked < fast_share, fast_rate, slow_rate)
    block_count = SEQUENCE_TOKENS // TOK_DEV
    block_multiplier = jnp.exp(jax.random.uniform(sample_sequences[2], (HEADS, block_count), dtype=jnp.float32, minval=jnp.log(0.5), maxval=jnp.log(2.0)))
    block_multiplier = jnp.repeat(block_multiplier, TOK_DEV, axis=1, total_repeat_length=SEQUENCE_TOKENS)
    jitter_amplitude = jax.random.uniform(sample_sequences[3], (HEADS, SEQUENCE_TOKENS), dtype=jnp.float32, minval=0.5, maxval=1.5)
    spike_locations = jax.random.randint(sample_sequences[4], (3,), 0, SEQUENCE_TOKENS)
    spike_magnitude = jax.random.uniform(sample_sequences[5], (HEADS, 3), dtype=jnp.float32, minval=0.22, maxval=0.69)
    decay_spikes = jnp.sum(jnp.where(token_position[None, :, None] == spike_locations[None, None, :], spike_magnitude[:, None, :], 0.0), axis=2)
    return (-(baseline_decay_rate * block_multiplier * jitter_amplitude + decay_spikes)).astype(jnp.float32)


def draw_value_rows(key, part):
    sample_sequences = jax.random.split(key, 3)
    head_number = (jnp.arange(HD) // DH).astype(jnp.float32)
    head_scale = 1.0 + 2.0 * head_number / max(HEADS - 1, 1)
    base = jnp.clip(jax.random.normal(sample_sequences[0], (SEQUENCE_TOKENS, HD), dtype=jnp.float32), -4.0, 4.0)
    row_scale = jnp.exp(jax.random.uniform(sample_sequences[2], (SEQUENCE_TOKENS, 1), dtype=jnp.float32, minval=0.0, maxval=jnp.log(10.0)))
    return (base * head_scale[None, :] * row_scale).astype(jnp.bfloat16)


def draw_grad_out(key, part):
    sample_sequences = jax.random.split(key, 1)
    ramp = 1.0 + 2.0 * jnp.arange(SEQUENCE_TOKENS).astype(jnp.float32) / (SEQUENCE_TOKENS - 1)
    base = jnp.clip(jax.random.normal(sample_sequences[0], (SEQUENCE_TOKENS, HD), dtype=jnp.float32), -4.0, 4.0)
    return (base * ramp[:, None]).astype(jnp.bfloat16)


def level_of(rng, dims, cuts, least, largest):
    def one(axis_at, parts):
        draws = jax.random.uniform(jax.random.fold_in(jax.random.fold_in(rng, 6), axis_at), (parts,), jnp.float32, least / len(cuts), largest / len(cuts))
        return jnp.repeat(jnp.exp(draws), dims[axis_at] // parts).reshape((-1,) + (1,) * (len(dims) - axis_at - 1))

    factor_of = one(*cuts[0])
    for cut in cuts[1:]:
        factor_of = factor_of * one(*cut)
    return factor_of


def normal_values(rng, extent, width, limit, cuts=(), held_as=jnp.bfloat16):
    result = jax.random.normal(rng, extent, jnp.float32) * width
    if len(cuts) > 0:
        result = level_of(rng, extent, cuts, -0.22, 0.18) * result
    return jnp.clip(result, min=-limit, max=limit).astype(held_as)


def setup_inputs(seed: int = 0) -> dict:
    arg_keys = jax.random.split(jax.random.key(seed), 7)
    queries = normal_values(arg_keys[0], (SEQUENCE_TOKENS, HD), 1.0, 6.0, ((0, 8), (1, 4)))
    key_rows = normal_values(arg_keys[1], (SEQUENCE_TOKENS, HD), DH ** -0.5, 0.5, ((0, 8), (1, 4)))
    value_rows = draw_value_rows(jax.random.fold_in(arg_keys[6], 71), 0)
    log_decay = draw_log_decay(jax.random.fold_in(arg_keys[6], 71), 0)
    norm_gain = jnp.clip(1.0 + 0.18 * jax.random.normal(arg_keys[4], (HD,), jnp.float32), 0.1, 1.9)
    grad_out = draw_grad_out(jax.random.fold_in(arg_keys[6], 71), 0)
    return dict(queries=queries, key_rows=key_rows, value_rows=value_rows, log_decay=log_decay, norm_gain=norm_gain, grad_out=grad_out)


EPSILON = 1e-06

def exact_product(form, left, right):
    return jnp.einsum(form, left.astype(jnp.float32), right.astype(jnp.float32), precision=lax.Precision.HIGHEST)

def plain_product(form, left, right):
    return jnp.einsum(form, left.astype(jnp.float32), right.astype(jnp.float32))

def causal_decay(cumulative):
    length = cumulative.shape[-1]
    below_diag = jnp.arange(length)[:, None] >= jnp.arange(length)[None, :]
    spread = cumulative[..., :, None] - cumulative[..., None, :]
    return jnp.where(below_diag, jnp.exp(jnp.where(below_diag, spread, 0.0)), 0.0)

def split_heads(matrix):
    return matrix.reshape(matrix.shape[0], HEADS, DH).transpose(1, 0, 2)

def merge_heads(tensor):
    return tensor.transpose(1, 0, 2).reshape(tensor.shape[1], HD)

def attend(q_heads, k_heads, v_heads, cumulative, state):
    decay_mask = causal_decay(cumulative)
    scores = plain_product('htd,hsd->hts', q_heads, k_heads)
    weights = (scores * decay_mask).astype(jnp.bfloat16)
    attended = plain_product('hts,hsd->htd', weights, v_heads)
    attended = attended + jnp.exp(cumulative)[..., None] * exact_product('htd,hde->hte', q_heads, state)
    return (attended, weights, decay_mask)

def normalize(attended, grad_rows, norm_gain):
    mixed = merge_heads(attended)
    inverse = lax.rsqrt(lax.optimization_barrier(jnp.mean(mixed * mixed, axis=1)) + EPSILON)
    normed = mixed * inverse[:, None]
    scaled = grad_rows.astype(jnp.float32) * norm_gain[None, :]
    center = lax.optimization_barrier(jnp.mean(scaled * normed, axis=1))
    grad_attended = (inverse[:, None] * (scaled - normed * center[:, None])).astype(jnp.bfloat16)
    return (normed, split_heads(grad_attended))

def reference(queries, key_rows, value_rows, log_decay, norm_gain, grad_out):
    blocks = SEQUENCE_TOKENS // TOK_DEV

    def tile(matrix):
        return matrix.reshape(blocks, TOK_DEV, HEADS, DH).transpose(0, 2, 1, 3)
    q_all = tile(queries)
    k_all = tile(key_rows)
    v_all = tile(value_rows)
    grad_rows = grad_out.reshape(blocks, TOK_DEV, HD)
    cumulative = jnp.cumsum(log_decay.reshape(HEADS, blocks, TOK_DEV).transpose(1, 0, 2), axis=2)
    block_total = cumulative[:, :, -1]

    def local_fn(operands):
        k_heads, v_heads, cumul, last_value = operands
        tail = jnp.exp(last_value[:, None] - cumul)
        return exact_product('htd,hte->hde', k_heads.astype(jnp.float32) * tail[..., None], v_heads)
    local_state = lax.map(local_fn, (k_all, v_all, cumulative, block_total))

    def carry_step(carry, operands):
        decay_total, local_term = operands
        return (decay_total[:, None, None] * carry + local_term, carry)
    zero_state = jnp.zeros((HEADS, DH, DH), jnp.float32)
    _, state_in = lax.scan(carry_step, zero_state, (jnp.exp(block_total), local_state))

    def second_pass(operands):
        q_heads, k_heads, v_heads, grad_block, cumul, state = operands
        attended, _, _ = attend(q_heads, k_heads, v_heads, cumul, state)
        normed, grad_heads = normalize(attended, grad_block, norm_gain)
        output_block = (normed * norm_gain[None, :]).astype(jnp.bfloat16)
        gain_part = lax.optimization_barrier(jnp.sum(grad_block.astype(jnp.float32) * normed, axis=0))
        state_grad = exact_product('htd,hte->hde', q_heads.astype(jnp.float32) * jnp.exp(cumul)[..., None], grad_heads)
        return (output_block, gain_part, state_grad)
    output, gain_parts, state_grad = lax.map(second_pass, (q_all, k_all, v_all, grad_rows, cumulative, state_in))
    _, state_after = lax.scan(carry_step, zero_state, (jnp.exp(block_total), state_grad), reverse=True)

    def fourth_pass(operands):
        q_heads, k_heads, v_heads, grad_block, cumul, last_value, state, after = operands
        attended, weights, decay_mask = attend(q_heads, k_heads, v_heads, cumul, state)
        _, grad_heads = normalize(attended, grad_block, norm_gain)
        grad_weights = (plain_product('htd,hsd->hts', grad_heads, v_heads) * decay_mask).astype(jnp.bfloat16)
        tail = jnp.exp(last_value[:, None] - cumul)[..., None]
        grad_q = plain_product('hts,hsd->htd', grad_weights, k_heads)
        grad_q = grad_q + jnp.exp(cumul)[..., None] * exact_product('hte,hde->htd', grad_heads, state)
        grad_k = plain_product('hts,htd->hsd', grad_weights, q_heads)
        grad_k = grad_k + tail * exact_product('hse,hde->hsd', v_heads, after)
        grad_v = plain_product('hts,htd->hsd', weights, grad_heads)
        grad_v = grad_v + tail * exact_product('hsd,hde->hse', k_heads, after)
        return (merge_heads(grad_q).astype(jnp.bfloat16), merge_heads(grad_k).astype(jnp.bfloat16), merge_heads(grad_v).astype(jnp.bfloat16))
    grad_q, grad_k, grad_v = lax.map(fourth_pass, (q_all, k_all, v_all, grad_rows, cumulative, block_total, state_in, state_after))
    grad_gain = lax.optimization_barrier(jnp.sum(gain_parts, axis=0))
    return (output.reshape(SEQUENCE_TOKENS, HD), grad_q.reshape(SEQUENCE_TOKENS, HD), grad_k.reshape(SEQUENCE_TOKENS, HD), grad_v.reshape(SEQUENCE_TOKENS, HD), grad_gain)
```

```python
import functools

import jax
import jax.numpy as jnp
from jax import lax
from jax.experimental import pallas as pl
from jax.experimental.pallas import tpu as pltpu
from jax.sharding import PartitionSpec as P

DH = 128
EPSILON = 1e-06
CHUNK = 256
F32 = jnp.float32
BF16 = jnp.bfloat16
MESH = pl.DeviceIdType.MESH
HIGHEST = lax.Precision.HIGHEST


def mm(left, right, dims):
    return lax.dot_general(left, right, (dims, ((), ())), preferred_element_type=F32)


AB = ((1,), (0,))
ABT = ((1,), (1,))
ATB = ((0,), (0,))


def chunk_cumsum(ld_ref, cum_ref, chunk):
    below = lax.broadcasted_iota(jnp.int32, (chunk, chunk), 0)
    right = lax.broadcasted_iota(jnp.int32, (chunk, chunk), 1)
    tri = (below <= right).astype(F32)
    for j in range(ld_ref.shape[1] // chunk):
        span = slice(j * chunk, (j + 1) * chunk)
        cum_ref[:, span] = lax.dot_general(
            ld_ref[:, span], tri, (AB, ((), ())), precision=HIGHEST, preferred_element_type=F32
        )


def cum_forms(cum_ref, h, j, chunk):
    row = cum_ref[pl.ds(h, 1), j * chunk : (j + 1) * chunk]
    column = jnp.broadcast_to(row, (DH, chunk)).T
    return row, column


def decay_of(row, column):
    chunk = row.shape[1]
    wide = jnp.concatenate([column] * (chunk // DH), axis=1)
    t = lax.broadcasted_iota(jnp.int32, (chunk, chunk), 0)
    s = lax.broadcasted_iota(jnp.int32, (chunk, chunk), 1)
    return jnp.where(t >= s, jnp.exp(wide - row), 0.0)


def remote(src, dst, send, recv, axis, target):
    return pltpu.make_async_remote_copy(
        src_ref=src, dst_ref=dst, send_sem=send, recv_sem=recv,
        device_id={axis: target}, device_id_type=MESH,
    )


def loop(count, body):
    lax.fori_loop(0, count, lambda i, c: (body(i), c)[1], 0)


class Chain:
    def __init__(self, n, reverse, bufs):
        (self.lsend, self.lrecv, self.zsend, self.zrecv, self.xsend, self.xrecv, self.sems) = bufs
        me = lax.axis_index("seq")
        self.partner = me + 1 - 2 * lax.rem(me, 2)
        place = n - 1 - me if reverse else me
        self.later = lax.rem(place, 2)
        self.row = place // 2
        self.first = self.row == 0
        self.last = self.row == n // 2 - 1
        step = -2 if reverse else 2
        self.next = lax.rem(me + step + n, n)

    def leads(self, h):
        return lax.rem(h, 2) != self.later

    def copy_l(self, h):
        return remote(self.lsend.at[h], self.lrecv.at[h], self.sems.at[0, h], self.sems.at[1, h], "seq", self.partner)

    def copy_x(self, h):
        return remote(self.xsend.at[h], self.xrecv.at[h], self.sems.at[2, h], self.sems.at[3, h], "seq", self.partner)

    def copy_z(self, h):
        return remote(self.zsend.at[h], self.zrecv.at[h], self.sems.at[4, h], self.sems.at[5, h], "seq", self.next)

    def start(self):
        @pl.when(self.first)
        def _():
            self.zrecv[...] = jnp.zeros_like(self.zrecv)

    def give(self, h, state, decay):
        self.lsend[h, 0:DH] = state
        self.lsend[h, DH : DH + 8] = jnp.broadcast_to(decay, (8, DH))

        @pl.when(jnp.logical_not(self.leads(h)))
        def _():
            self.copy_l(h).start()

    def step(self, h, state_in):
        @pl.when(self.leads(h))
        def _():
            self.copy_l(h).wait_recv()

            @pl.when(jnp.logical_not(self.first))
            def _():
                self.copy_z(h).wait_recv()

            state = self.zrecv[h]

            @pl.when(self.later == 1)
            def _():
                mid = self.lrecv[h, DH : DH + 1] * state + self.lrecv[h, 0:DH]
                self.xsend[h] = state
                self.copy_x(h).start()
                self.zsend[h] = self.lsend[h, DH : DH + 1] * mid + self.lsend[h, 0:DH]
                state_in[h] = mid

            @pl.when(self.later == 0)
            def _():
                mid = self.lsend[h, DH : DH + 1] * state + self.lsend[h, 0:DH]
                self.xsend[h] = mid
                self.copy_x(h).start()
                self.zsend[h] = self.lrecv[h, DH : DH + 1] * mid + self.lrecv[h, 0:DH]
                state_in[h] = state

            @pl.when(jnp.logical_not(self.last))
            def _():
                self.copy_z(h).start()

    def take(self, h, state_in):
        @pl.when(jnp.logical_not(self.leads(h)))
        def _():
            self.copy_x(h).wait_recv()
            state_in[h] = self.xrecv[h]

    def finish(self, h):
        @pl.when(self.leads(h))
        def _():
            self.copy_x(h).wait_send()

            @pl.when(jnp.logical_not(self.last))
            def _():
                self.copy_z(h).wait_send()

        @pl.when(jnp.logical_not(self.leads(h)))
        def _():
            self.copy_l(h).wait_send()


def main_kernel(
    n, peers, chunk,
    q_hbm, k_hbm, v_hbm, g_hbm, ld_ref, gain_ref,
    grad_hbm, out_hbm, s_out, r_out, gg_out,
    q, k, v, g, att, obuf, cum_ref, lc, state_in, sq_acc, in_acc,
    stat_send, stat_recv, gain_send, gain_recv, inv_b, cen_b,
    lsend1, lrecv1, zsend1, zrecv1, xsend1, xrecv1,
    lsend2, lrecv2, zsend2, zrecv2, xsend2, xrecv2,
    load_sem, store_sem, chain1_sem, chain2_sem, stat_sem, gain_sem,
):
    heads, tokens, _ = q.shape
    chunks = tokens // chunk
    me = lax.axis_index("seq")
    my_head = lax.axis_index("head")
    columns = heads * DH * peers

    def load(i, hbm, vmem, h):
        where = pl.ds(pl.multiple_of(h * DH, DH), DH)
        return pltpu.make_async_copy(hbm.at[:, where], vmem.at[h], load_sem.at[i, h])

    def store(i, vmem, hbm, h):
        where = pl.ds(pl.multiple_of(h * DH, DH), DH)
        return pltpu.make_async_copy(vmem.at[h], hbm.at[:, where], store_sem.at[i, h])

    def load_kv(h):
        load(0, k_hbm, k, h).start()
        load(1, v_hbm, v, h).start()

    def load_q(h):
        load(2, q_hbm, q, h).start()

    def load_g(h):
        load(3, g_hbm, g, h).start()

    loop(heads, load_kv)
    loop(heads, load_q)
    loop(heads, load_g)

    barrier = pltpu.get_barrier_semaphore()
    for off in range(1, n):
        pl.semaphore_signal(barrier, inc=1, device_id={"seq": lax.rem(me + off, n)}, device_id_type=MESH)
    for off in range(1, peers):
        pl.semaphore_signal(barrier, inc=1, device_id={"head": lax.rem(my_head + off, peers)}, device_id_type=MESH)
    chunk_cumsum(ld_ref, cum_ref, chunk)
    forward = Chain(n, False, (lsend1, lrecv1, zsend1, zrecv1, xsend1, xrecv1, chain1_sem))
    backward = Chain(n, True, (lsend2, lrecv2, zsend2, zrecv2, xsend2, xrecv2, chain2_sem))
    forward.start()
    backward.start()
    pl.semaphore_wait(barrier, n - 1 + peers - 1)

    def local_state(h):
        load(0, k_hbm, k, h).wait()
        load(1, v_hbm, v, h).wait()
        state = None
        for j in range(chunks):
            span = slice(j * chunk, (j + 1) * chunk)
            _, column = cum_forms(cum_ref, h, j, chunk)
            total = column[chunk - 1 : chunk, :]
            tail = jnp.exp(total - column)
            part = mm((k[h, span].astype(F32) * tail).astype(BF16), v[h, span], ATB)
            lc[h, j] = part
            state = part if j == 0 else jnp.exp(total) * state + part
            decay = total if j == 0 else decay + total
        forward.give(h, state, jnp.exp(decay))

    loop(heads, local_state)

    def intra(h):
        load(2, q_hbm, q, h).wait()
        for j in range(chunks):
            span = slice(j * chunk, (j + 1) * chunk)
            row, column = cum_forms(cum_ref, h, j, chunk)
            scores = mm(q[h, span], k[h, span], ABT)
            weights = (scores * decay_of(row, column)).astype(BF16)
            att[h, span] = mm(weights, v[h, span], AB)

    lag = forward.row * 2 + 1

    def overlap(i):
        @pl.when(i < heads)
        def _():
            intra(i)

        at = i - lag

        @pl.when(jnp.logical_and(at >= 0, at < heads))
        def _():
            forward.step(at, state_in)

    loop(heads + n, overlap)

    sq_acc[...] = jnp.zeros_like(sq_acc)
    in_acc[...] = jnp.zeros_like(in_acc)

    def inter(h):
        load(3, g_hbm, g, h).wait()
        forward.take(h, state_in)
        state = state_in[h]
        gain = gain_ref[pl.ds(h, 1), :]
        for j in range(chunks):
            span = slice(j * chunk, (j + 1) * chunk)
            _, column = cum_forms(cum_ref, h, j, chunk)
            rounded = state.astype(BF16)
            s_out[h, j] = rounded
            whole = att[h, span] + jnp.exp(column) * mm(q[h, span], rounded, AB)
            att[h, span] = whole
            sq_acc[span] += whole * whole
            in_acc[span] += g[h, span].astype(F32) * gain * whole
            if j < chunks - 1:
                state = jnp.exp(column[chunk - 1 : chunk, :]) * state + lc[h, j]

    loop(heads, inter)

    ones = jnp.ones((8, DH), F32)

    def row_sums(acc):
        return lax.dot_general(ones, acc, (ABT, ((), ())), precision=HIGHEST, preferred_element_type=F32)

    upper = lax.broadcasted_iota(jnp.int32, (8, tokens), 0) < 4
    stat_send[...] = jnp.where(upper, row_sums(sq_acc[...]), row_sums(in_acc[...]))

    def stat_copy(off, slot):
        return remote(stat_send, stat_recv.at[slot], stat_sem.at[0, off], stat_sem.at[1, off], "head", lax.rem(my_head + off, peers))

    for off in range(1, peers):
        stat_copy(off, my_head).start()
    stat_recv[my_head] = stat_send[...]
    for off in range(1, peers):
        stat_copy(off, lax.rem(my_head + peers - off, peers)).wait_recv()
    stats = stat_recv[0]
    for i in range(1, peers):
        stats = stats + stat_recv[i]
    inverse = lax.rsqrt(stats[0:1] / columns + EPSILON)
    center = stats[4:5] * inverse / columns
    inv_b[...] = jnp.broadcast_to(inverse, (DH, tokens)).T
    cen_b[...] = jnp.broadcast_to(center, (DH, tokens)).T

    def normalize(h):
        gain = gain_ref[pl.ds(h, 1), :]
        gain_part = jnp.zeros((1, DH), F32)
        state = None
        for j in reversed(range(chunks)):
            span = slice(j * chunk, (j + 1) * chunk)
            _, column = cum_forms(cum_ref, h, j, chunk)
            normed = att[h, span] * inv_b[span]
            obuf[h, span] = (normed * gain).astype(BF16)
            cotangent = g[h, span].astype(F32)
            gain_part = gain_part + jnp.sum(cotangent * normed, axis=0, keepdims=True)
            grad = (inv_b[span] * (cotangent * gain - normed * cen_b[span])).astype(BF16)
            g[h, span] = grad
            part = mm((q[h, span].astype(F32) * jnp.exp(column)).astype(BF16), grad, ATB)
            lc[h, j] = part
            total = column[chunk - 1 : chunk, :]
            state = part if state is None else jnp.exp(total) * state + part
            decay = total if j == chunks - 1 else decay + total
        backward.give(h, state, jnp.exp(decay))
        gain_send[pl.ds(h, 1), :] = gain_part
        store(0, g, grad_hbm, h).start()
        store(1, obuf, out_hbm, h).start()

    loop(heads, normalize)

    def gain_copy(off, slot):
        return remote(gain_send, gain_recv.at[slot], gain_sem.at[0, off], gain_sem.at[1, off], "seq", lax.rem(me + off, n))

    for off in range(1, n):
        gain_copy(off, me).start()
    gain_recv[me] = gain_send[...]

    loop(heads, lambda h: backward.step(h, state_in))

    def after(h):
        backward.take(h, state_in)
        state = state_in[h]
        for j in reversed(range(chunks)):
            r_out[h, j] = state.astype(BF16)
            if j > 0:
                _, column = cum_forms(cum_ref, h, j, chunk)
                state = jnp.exp(column[chunk - 1 : chunk, :]) * state + lc[h, j]

    loop(heads, after)

    for off in range(1, n):
        gain_copy(off, lax.rem(me + n - off, n)).wait_recv()
    gain_total = gain_recv[0]
    for i in range(1, n):
        gain_total = gain_total + gain_recv[i]
    gg_out[...] = gain_total

    def finish(h):
        forward.finish(h)
        backward.finish(h)
        store(0, g, grad_hbm, h).wait()
        store(1, obuf, out_hbm, h).wait()

    loop(heads, finish)
    for off in range(1, peers):
        stat_copy(off, my_head).wait_send()
    for off in range(1, n):
        gain_copy(off, me).wait_send()


def backward_kernel(
    chunk, q_ref, k_ref, v_ref, grad_ref, pass_ref, ld_ref, s_ref, r_ref,
    out_ref, gq_ref, gk_ref, gv_ref, cum_ref,
):
    h = pl.program_id(0)
    tokens = q_ref.shape[0]

    @pl.when(h == 0)
    def _():
        chunk_cumsum(ld_ref, cum_ref, chunk)

    out_ref[...] = pass_ref[...]
    for j in range(tokens // chunk):
        span = slice(j * chunk, (j + 1) * chunk)
        row, column = cum_forms(cum_ref, h, j, chunk)
        decay = decay_of(row, column)
        growth = jnp.exp(column)
        tail = jnp.exp(column[chunk - 1 : chunk, :] - column)
        q, k, v, grad = q_ref[span], k_ref[span], v_ref[span], grad_ref[span]
        weights = (mm(q, k, ABT) * decay).astype(BF16)
        grad_weights = (mm(grad, v, ABT) * decay).astype(BF16)
        state, after = s_ref[0, j], r_ref[0, j]
        gq_ref[span] = (mm(grad_weights, k, AB) + growth * mm(grad, state, ABT)).astype(BF16)
        gk_ref[span] = (mm(grad_weights, q, ATB) + tail * mm(v, after, ABT)).astype(BF16)
        gv_ref[span] = (mm(weights, grad, ATB) + tail * mm(k, after, AB)).astype(BF16)


def on_device(n, peers, queries, key_rows, value_rows, log_decay, norm_gain, grad_out):
    tokens, width = queries.shape
    heads = width // DH
    chunk = CHUNK if tokens % CHUNK == 0 else tokens
    chunks = tokens // chunk
    gain = norm_gain.reshape(heads, DH)
    anywhere = pl.BlockSpec(memory_space=pl.ANY)
    vmem = pl.BlockSpec(memory_space=pltpu.VMEM)
    rows = jax.ShapeDtypeStruct((tokens, width), BF16)
    states = jax.ShapeDtypeStruct((heads, chunks, DH, DH), BF16)
    per_head = lambda *shape, dtype=F32: pltpu.VMEM((heads, *shape), dtype)
    chain = [
        per_head(DH + 8, DH), per_head(DH + 8, DH), per_head(DH, DH),
        per_head(DH, DH), per_head(DH, DH), per_head(DH, DH),
    ]
    dma = pltpu.SemaphoreType.DMA
    grad, out, state, after, grad_gain = pl.pallas_call(
        functools.partial(main_kernel, n, peers, chunk),
        out_shape=(rows, rows, states, states, jax.ShapeDtypeStruct((heads, DH), F32)),
        in_specs=[anywhere] * 4 + [vmem] * 2,
        out_specs=(anywhere, anywhere, vmem, vmem, vmem),
        scratch_shapes=[
            per_head(tokens, DH, dtype=BF16), per_head(tokens, DH, dtype=BF16),
            per_head(tokens, DH, dtype=BF16), per_head(tokens, DH, dtype=BF16),
            per_head(tokens, DH), per_head(tokens, DH, dtype=BF16),
            pltpu.VMEM((heads, tokens), F32), per_head(chunks, DH, DH), per_head(DH, DH),
            pltpu.VMEM((tokens, DH), F32), pltpu.VMEM((tokens, DH), F32),
            pltpu.VMEM((8, tokens), F32), pltpu.VMEM((peers, 8, tokens), F32),
            pltpu.VMEM((heads, DH), F32), pltpu.VMEM((n, heads, DH), F32),
            pltpu.VMEM((tokens, DH), F32), pltpu.VMEM((tokens, DH), F32),
            *chain, *chain,
            dma((4, heads)), dma((2, heads)), dma((6, heads)), dma((6, heads)),
            dma((2, peers)), dma((2, n)),
        ],
        compiler_params=pltpu.CompilerParams(
            collective_id=0, has_side_effects=True, vmem_limit_bytes=60 * 1024 * 1024
        ),
        name="forward_chain",
    )(queries, key_rows, value_rows, grad_out, log_decay, gain)
    block = pl.BlockSpec((tokens, DH), lambda h: (0, h))
    per_state = pl.BlockSpec((1, chunks, DH, DH), lambda h: (h, 0, 0, 0))
    out, grad_q, grad_k, grad_v = pl.pallas_call(
        functools.partial(backward_kernel, chunk),
        grid=(heads,),
        out_shape=(rows,) * 4,
        in_specs=[block] * 5 + [pl.BlockSpec((heads, tokens), lambda h: (0, 0)), per_state, per_state],
        out_specs=(block,) * 4,
        scratch_shapes=[pltpu.VMEM((heads, tokens), F32)],
        name="backward_heads",
    )(queries, key_rows, value_rows, grad, out, log_decay, state, after)
    return out, grad_q, grad_k, grad_v, grad_gain.reshape(width)


def solution(mesh):
    in_specs = (
        P("seq", "head"),
        P("seq", "head"),
        P("seq", "head"),
        P("head", "seq"),
        P("head"),
        P("seq", "head"),
    )
    out_specs = (P("seq", "head"), P("seq", "head"), P("seq", "head"), P("seq", "head"), P("head"))
    return jax.shard_map(
        functools.partial(on_device, mesh.shape["seq"], mesh.shape["head"]),
        mesh=mesh, in_specs=in_specs, out_specs=out_specs, check_vma=False,
    )
```

```python
import functools

import jax
import jax.numpy as jnp
from jax import lax
from jax.experimental import pallas as pl
from jax.experimental.pallas import tpu as pltpu
from jax.sharding import PartitionSpec as P

DH = 128
EPSILON = 1e-06
CHUNK = 256
F32 = jnp.float32
BF16 = jnp.bfloat16
MESH = pl.DeviceIdType.MESH
HIGHEST = lax.Precision.HIGHEST


def mm(left, right, dims):
    return lax.dot_general(left, right, (dims, ((), ())), preferred_element_type=F32)


AB = ((1,), (0,))
ABT = ((1,), (1,))
ATB = ((0,), (0,))


def chunk_cumsum(ld_ref, cum_ref, chunk):
    below = lax.broadcasted_iota(jnp.int32, (chunk, chunk), 0)
    right = lax.broadcasted_iota(jnp.int32, (chunk, chunk), 1)
    tri = (below <= right).astype(F32)
    for j in range(ld_ref.shape[1] // chunk):
        span = slice(j * chunk, (j + 1) * chunk)
        cum_ref[:, span] = lax.dot_general(
            ld_ref[:, span], tri, (AB, ((), ())), precision=HIGHEST, preferred_element_type=F32
        )


def cum_forms(cum_ref, h, j, chunk):
    row = cum_ref[pl.ds(h, 1), j * chunk : (j + 1) * chunk]
    column = jnp.broadcast_to(row, (DH, chunk)).T
    return row, column


def decay_of(row, column):
    chunk = row.shape[1]
    wide = jnp.concatenate([column] * (chunk // DH), axis=1)
    t = lax.broadcasted_iota(jnp.int32, (chunk, chunk), 0)
    s = lax.broadcasted_iota(jnp.int32, (chunk, chunk), 1)
    return jnp.where(t >= s, jnp.exp(wide - row), 0.0)


def remote(src, dst, send, recv, axis, target):
    return pltpu.make_async_remote_copy(
        src_ref=src, dst_ref=dst, send_sem=send, recv_sem=recv,
        device_id={axis: target}, device_id_type=MESH,
    )


def loop(count, body):
    lax.fori_loop(0, count, lambda i, c: (body(i), c)[1], 0)


class Chain:
    def __init__(self, n, reverse, bufs):
        (self.lsend, self.lrecv, self.zsend, self.zrecv, self.xsend, self.xrecv, self.sems) = bufs
        me = lax.axis_index("seq")
        self.partner = me + 1 - 2 * lax.rem(me, 2)
        place = n - 1 - me if reverse else me
        self.later = lax.rem(place, 2)
        self.row = place // 2
        self.first = self.row == 0
        self.last = self.row == n // 2 - 1
        step = -2 if reverse else 2
        self.next = lax.rem(me + step + n, n)

    def leads(self, h):
        return lax.rem(h, 2) != self.later

    def copy_l(self, h):
        return remote(self.lsend.at[h], self.lrecv.at[h], self.sems.at[0, h], self.sems.at[1, h], "seq", self.partner)

    def copy_x(self, h):
        return remote(self.xsend.at[h], self.xrecv.at[h], self.sems.at[2, h], self.sems.at[3, h], "seq", self.partner)

    def copy_z(self, h):
        return remote(self.zsend.at[h], self.zrecv.at[h], self.sems.at[4, h], self.sems.at[5, h], "seq", self.next)

    def start(self):
        @pl.when(self.first)
        def _():
            self.zrecv[...] = jnp.zeros_like(self.zrecv)

    def give(self, h, state, decay):
        self.lsend[h, 0:DH] = state
        self.lsend[h, DH : DH + 8] = jnp.broadcast_to(decay, (8, DH))

        @pl.when(jnp.logical_not(self.leads(h)))
        def _():
            self.copy_l(h).start()

    def step(self, h, state_in):
        @pl.when(self.leads(h))
        def _():
            self.copy_l(h).wait_recv()

            @pl.when(jnp.logical_not(self.first))
            def _():
                self.copy_z(h).wait_recv()

            state = self.zrecv[h]

            @pl.when(self.later == 1)
            def _():
                mid = self.lrecv[h, DH : DH + 1] * state + self.lrecv[h, 0:DH]
                self.xsend[h] = state
                self.copy_x(h).start()
                self.zsend[h] = self.lsend[h, DH : DH + 1] * mid + self.lsend[h, 0:DH]
                state_in[h] = mid

            @pl.when(self.later == 0)
            def _():
                mid = self.lsend[h, DH : DH + 1] * state + self.lsend[h, 0:DH]
                self.xsend[h] = mid
                self.copy_x(h).start()
                self.zsend[h] = self.lrecv[h, DH : DH + 1] * mid + self.lrecv[h, 0:DH]
                state_in[h] = state

            @pl.when(jnp.logical_not(self.last))
            def _():
                self.copy_z(h).start()

    def take(self, h, state_in):
        @pl.when(jnp.logical_not(self.leads(h)))
        def _():
            self.copy_x(h).wait_recv()
            state_in[h] = self.xrecv[h]

    def finish(self, h):
        @pl.when(self.leads(h))
        def _():
            self.copy_x(h).wait_send()

            @pl.when(jnp.logical_not(self.last))
            def _():
                self.copy_z(h).wait_send()

        @pl.when(jnp.logical_not(self.leads(h)))
        def _():
            self.copy_l(h).wait_send()


def main_kernel(
    n, peers, chunk,
    q_hbm, k_hbm, v_hbm, g_hbm, ld_ref, gain_ref,
    q, k, v, g, att, obuf, r_out, cum_ref, gg_out,
    s_out, lc, state_in, sq_acc, in_acc,
    stat_send, stat_recv, gain_send, gain_recv, inv_b, cen_b,
    lsend1, lrecv1, zsend1, zrecv1, xsend1, xrecv1,
    lsend2, lrecv2, zsend2, zrecv2, xsend2, xrecv2,
    load_sem, chain1_sem, chain2_sem, stat_sem, gain_sem,
):
    heads, tokens, _ = q.shape
    chunks = tokens // chunk
    me = lax.axis_index("seq")
    my_head = lax.axis_index("head")
    columns = heads * DH * peers

    def load(i, hbm, vmem, h):
        where = pl.ds(pl.multiple_of(h * DH, DH), DH)
        return pltpu.make_async_copy(hbm.at[:, where], vmem.at[h], load_sem.at[i, h])

    def load_kv(h):
        load(0, k_hbm, k, h).start()
        load(1, v_hbm, v, h).start()

    def load_q(h):
        load(2, q_hbm, q, h).start()

    def load_g(h):
        load(3, g_hbm, g, h).start()

    loop(heads, load_kv)
    loop(heads, load_q)
    loop(heads, load_g)

    barrier = pltpu.get_barrier_semaphore()
    for off in range(1, n):
        pl.semaphore_signal(barrier, inc=1, device_id={"seq": lax.rem(me + off, n)}, device_id_type=MESH)
    for off in range(1, peers):
        pl.semaphore_signal(barrier, inc=1, device_id={"head": lax.rem(my_head + off, peers)}, device_id_type=MESH)
    chunk_cumsum(ld_ref, cum_ref, chunk)
    forward = Chain(n, False, (lsend1, lrecv1, zsend1, zrecv1, xsend1, xrecv1, chain1_sem))
    backward = Chain(n, True, (lsend2, lrecv2, zsend2, zrecv2, xsend2, xrecv2, chain2_sem))
    forward.start()
    backward.start()
    pl.semaphore_wait(barrier, n - 1 + peers - 1)

    def local_state(h):
        load(0, k_hbm, k, h).wait()
        load(1, v_hbm, v, h).wait()
        state = None
        for j in range(chunks):
            span = slice(j * chunk, (j + 1) * chunk)
            _, column = cum_forms(cum_ref, h, j, chunk)
            total = column[chunk - 1 : chunk, :]
            tail = jnp.exp(total - column)
            part = mm((k[h, span].astype(F32) * tail).astype(BF16), v[h, span], ATB)
            lc[h, j] = part
            state = part if j == 0 else jnp.exp(total) * state + part
            decay = total if j == 0 else decay + total
        forward.give(h, state, jnp.exp(decay))

    loop(heads, local_state)

    def intra(h):
        load(2, q_hbm, q, h).wait()
        for j in range(chunks):
            span = slice(j * chunk, (j + 1) * chunk)
            row, column = cum_forms(cum_ref, h, j, chunk)
            scores = mm(q[h, span], k[h, span], ABT)
            weights = (scores * decay_of(row, column)).astype(BF16)
            att[h, span] = mm(weights, v[h, span], AB)

    lag = forward.row * 2 + 1

    def overlap(i):
        @pl.when(i < heads)
        def _():
            intra(i)

        at = i - lag

        @pl.when(jnp.logical_and(at >= 0, at < heads))
        def _():
            forward.step(at, state_in)

    loop(heads + n, overlap)

    sq_acc[...] = jnp.zeros_like(sq_acc)
    in_acc[...] = jnp.zeros_like(in_acc)

    def inter(h):
        load(3, g_hbm, g, h).wait()
        forward.take(h, state_in)
        state = state_in[h]
        gain = gain_ref[pl.ds(h, 1), :]
        for j in range(chunks):
            span = slice(j * chunk, (j + 1) * chunk)
            _, column = cum_forms(cum_ref, h, j, chunk)
            rounded = state.astype(BF16)
            s_out[h, j] = rounded
            whole = att[h, span] + jnp.exp(column) * mm(q[h, span], rounded, AB)
            att[h, span] = whole
            sq_acc[span] += whole * whole
            in_acc[span] += g[h, span].astype(F32) * gain * whole
            if j < chunks - 1:
                state = jnp.exp(column[chunk - 1 : chunk, :]) * state + lc[h, j]

    loop(heads, inter)

    ones = jnp.ones((8, DH), F32)

    def row_sums(acc):
        return lax.dot_general(ones, acc, (ABT, ((), ())), precision=HIGHEST, preferred_element_type=F32)

    upper = lax.broadcasted_iota(jnp.int32, (8, tokens), 0) < 4
    stat_send[...] = jnp.where(upper, row_sums(sq_acc[...]), row_sums(in_acc[...]))

    def stat_copy(off, slot):
        return remote(stat_send, stat_recv.at[slot], stat_sem.at[0, off], stat_sem.at[1, off], "head", lax.rem(my_head + off, peers))

    for off in range(1, peers):
        stat_copy(off, my_head).start()
    stat_recv[my_head] = stat_send[...]
    for off in range(1, peers):
        stat_copy(off, lax.rem(my_head + peers - off, peers)).wait_recv()
    stats = stat_recv[0]
    for i in range(1, peers):
        stats = stats + stat_recv[i]
    inverse = lax.rsqrt(stats[0:1] / columns + EPSILON)
    center = stats[4:5] * inverse / columns
    inv_b[...] = jnp.broadcast_to(inverse, (DH, tokens)).T
    cen_b[...] = jnp.broadcast_to(center, (DH, tokens)).T

    def normalize(h):
        gain = gain_ref[pl.ds(h, 1), :]
        gain_part = jnp.zeros((1, DH), F32)
        state = None
        for j in reversed(range(chunks)):
            span = slice(j * chunk, (j + 1) * chunk)
            _, column = cum_forms(cum_ref, h, j, chunk)
            normed = att[h, span] * inv_b[span]
            obuf[h, span] = (normed * gain).astype(BF16)
            cotangent = g[h, span].astype(F32)
            gain_part = gain_part + jnp.sum(cotangent * normed, axis=0, keepdims=True)
            grad = (inv_b[span] * (cotangent * gain - normed * cen_b[span])).astype(BF16)
            g[h, span] = grad
            part = mm((q[h, span].astype(F32) * jnp.exp(column)).astype(BF16), grad, ATB)
            lc[h, j] = part
            total = column[chunk - 1 : chunk, :]
            state = part if state is None else jnp.exp(total) * state + part
            decay = total if j == chunks - 1 else decay + total
        backward.give(h, state, jnp.exp(decay))
        gain_send[pl.ds(h, 1), :] = gain_part

    loop(heads, normalize)

    def gain_copy(off, slot):
        return remote(gain_send, gain_recv.at[slot], gain_sem.at[0, off], gain_sem.at[1, off], "seq", lax.rem(me + off, n))

    for off in range(1, n):
        gain_copy(off, me).start()
    gain_recv[me] = gain_send[...]

    def gradients(h):
        for j in range(chunks):
            span = slice(j * chunk, (j + 1) * chunk)
            row, column = cum_forms(cum_ref, h, j, chunk)
            decay = decay_of(row, column)
            queries, keys, values, grad = q[h, span], k[h, span], v[h, span], g[h, span]
            weights = (mm(queries, keys, ABT) * decay).astype(BF16)
            grad_weights = (mm(grad, values, ABT) * decay).astype(BF16)
            q[h, span] = (
                mm(grad_weights, keys, AB) + jnp.exp(column) * mm(grad, s_out[h, j], ABT)
            ).astype(BF16)
            att[h, span] = mm(grad_weights, queries, ATB)
            g[h, span] = mm(weights, grad, ATB).astype(BF16)

    back_lag = backward.row * 2 + 1

    def overlap_back(i):
        at = i - back_lag

        @pl.when(jnp.logical_and(at >= 0, at < heads))
        def _():
            backward.step(at, state_in)

        @pl.when(i < heads)
        def _():
            gradients(i)

    loop(heads + n, overlap_back)

    def after(h):
        backward.take(h, state_in)
        state = state_in[h]
        for j in reversed(range(chunks)):
            r_out[h, j] = state.astype(BF16)
            if j > 0:
                _, column = cum_forms(cum_ref, h, j, chunk)
                state = jnp.exp(column[chunk - 1 : chunk, :]) * state + lc[h, j]

    loop(heads, after)

    for off in range(1, n):
        gain_copy(off, lax.rem(me + n - off, n)).wait_recv()
    gain_total = gain_recv[0]
    for i in range(1, n):
        gain_total = gain_total + gain_recv[i]
    gg_out[...] = gain_total

    def finish(h):
        forward.finish(h)
        backward.finish(h)

    loop(heads, finish)
    for off in range(1, peers):
        stat_copy(off, my_head).wait_send()
    for off in range(1, n):
        gain_copy(off, me).wait_send()


def last_kernel(
    chunk, k, v, gq, gk, gv, out, after, cum_ref,
    out_hbm, gq_hbm, gk_hbm, gv_hbm, k_stage, v_stage, store_sem,
):
    heads, tokens, _ = k.shape

    def store(i, vmem, hbm, h):
        where = pl.ds(pl.multiple_of(h * DH, DH), DH)
        return pltpu.make_async_copy(vmem.at[h], hbm.at[:, where], store_sem.at[i, h])

    def copies(h):
        return (
            store(0, out, out_hbm, h), store(1, gq, gq_hbm, h),
            store(2, k_stage, gk_hbm, h), store(3, v_stage, gv_hbm, h),
        )

    def one(h):
        ready = copies(h)
        ready[0].start()
        ready[1].start()
        for j in range(tokens // chunk):
            span = slice(j * chunk, (j + 1) * chunk)
            _, column = cum_forms(cum_ref, h, j, chunk)
            tail = jnp.exp(column[chunk - 1 : chunk, :] - column)
            k_stage[h, span] = (gk[h, span] + tail * mm(v[h, span], after[h, j], ABT)).astype(BF16)
            v_stage[h, span] = (
                gv[h, span].astype(F32) + tail * mm(k[h, span], after[h, j], AB)
            ).astype(BF16)
        ready[2].start()
        ready[3].start()

    def wait(h):
        for copy in copies(h):
            copy.wait()

    loop(heads, one)
    loop(heads, wait)


def on_device(n, peers, queries, key_rows, value_rows, log_decay, norm_gain, grad_out):
    tokens, width = queries.shape
    heads = width // DH
    chunk = CHUNK if tokens % CHUNK == 0 else tokens
    chunks = tokens // chunk
    gain = norm_gain.reshape(heads, DH)
    anywhere = pl.BlockSpec(memory_space=pl.ANY)
    vmem = pl.BlockSpec(memory_space=pltpu.VMEM)
    rows = jax.ShapeDtypeStruct((tokens, width), BF16)
    states = jax.ShapeDtypeStruct((heads, chunks, DH, DH), BF16)
    per_head = lambda *shape, dtype=F32: pltpu.VMEM((heads, *shape), dtype)
    chain = [
        per_head(DH + 8, DH), per_head(DH + 8, DH), per_head(DH, DH),
        per_head(DH, DH), per_head(DH, DH), per_head(DH, DH),
    ]
    dma = pltpu.SemaphoreType.DMA
    by_head = lambda dtype: pltpu.VMEM((heads, tokens, DH), dtype)
    *held, grad_gain = pl.pallas_call(
        functools.partial(main_kernel, n, peers, chunk),
        out_shape=(
            by_head(BF16), by_head(BF16), by_head(BF16), by_head(BF16), by_head(F32), by_head(BF16),
            pltpu.VMEM((heads, chunks, DH, DH), BF16), pltpu.VMEM((heads, tokens), F32),
            jax.ShapeDtypeStruct((heads, DH), F32),
        ),
        in_specs=[anywhere] * 4 + [vmem] * 2,
        out_specs=(vmem,) * 9,
        scratch_shapes=[
            per_head(chunks, DH, DH, dtype=BF16), per_head(chunks, DH, DH), per_head(DH, DH),
            pltpu.VMEM((tokens, DH), F32), pltpu.VMEM((tokens, DH), F32),
            pltpu.VMEM((8, tokens), F32), pltpu.VMEM((peers, 8, tokens), F32),
            pltpu.VMEM((heads, DH), F32), pltpu.VMEM((n, heads, DH), F32),
            pltpu.VMEM((tokens, DH), F32), pltpu.VMEM((tokens, DH), F32),
            *chain, *chain,
            dma((4, heads)), dma((6, heads)), dma((6, heads)),
            dma((2, peers)), dma((2, n)),
        ],
        compiler_params=pltpu.CompilerParams(
            collective_id=0, has_side_effects=True, vmem_limit_bytes=32 * 1024 * 1024
        ),
        name="forward_chain",
    )(queries, key_rows, value_rows, grad_out, log_decay, gain)
    grad_q, key_held, value_held, grad_v, grad_k, out, after, cumulative = held
    out, grad_q, grad_k, grad_v = pl.pallas_call(
        functools.partial(last_kernel, chunk),
        out_shape=(rows,) * 4,
        in_specs=[vmem] * 8,
        out_specs=(anywhere,) * 4,
        scratch_shapes=[
            per_head(tokens, DH, dtype=BF16), per_head(tokens, DH, dtype=BF16), dma((4, heads)),
        ],
        compiler_params=pltpu.CompilerParams(vmem_limit_bytes=16 * 1024 * 1024),
        name="last_terms",
    )(key_held, value_held, grad_q, grad_k, grad_v, out, after, cumulative)
    return out, grad_q, grad_k, grad_v, grad_gain.reshape(width)


def solution(mesh):
    in_specs = (
        P("seq", "head"),
        P("seq", "head"),
        P("seq", "head"),
        P("head", "seq"),
        P("head"),
        P("seq", "head"),
    )
    out_specs = (P("seq", "head"), P("seq", "head"), P("seq", "head"), P("seq", "head"), P("head"))
    return jax.shard_map(
        functools.partial(on_device, mesh.shape["seq"], mesh.shape["head"]),
        mesh=mesh, in_specs=in_specs, out_specs=out_specs, check_vma=False,
    )
```

```python
import functools

import jax
import jax.numpy as jnp
from jax import lax
from jax.experimental import pallas as pl
from jax.experimental.pallas import tpu as pltpu
from jax.sharding import PartitionSpec as P

DH = 128
EPSILON = 1e-06
CHUNK = 256
F32 = jnp.float32
BF16 = jnp.bfloat16
MESH = pl.DeviceIdType.MESH
HIGHEST = lax.Precision.HIGHEST


def mm(left, right, dims):
    return lax.dot_general(left, right, (dims, ((), ())), preferred_element_type=F32)


AB = ((1,), (0,))
ABT = ((1,), (1,))
ATB = ((0,), (0,))


def chunk_cumsum(ld_ref, cum_ref, chunk):
    below = lax.broadcasted_iota(jnp.int32, (chunk, chunk), 0)
    right = lax.broadcasted_iota(jnp.int32, (chunk, chunk), 1)
    tri = (below <= right).astype(F32)
    for j in range(ld_ref.shape[1] // chunk):
        span = slice(j * chunk, (j + 1) * chunk)
        cum_ref[:, span] = lax.dot_general(
            ld_ref[:, span], tri, (AB, ((), ())), precision=HIGHEST, preferred_element_type=F32
        )


def cum_forms(cum_ref, h, j, chunk):
    row = cum_ref[pl.ds(h, 1), j * chunk : (j + 1) * chunk]
    column = jnp.broadcast_to(row, (DH, chunk)).T
    return row, column


def decay_of(row, column):
    chunk = row.shape[1]
    wide = jnp.concatenate([column] * (chunk // DH), axis=1)
    t = lax.broadcasted_iota(jnp.int32, (chunk, chunk), 0)
    s = lax.broadcasted_iota(jnp.int32, (chunk, chunk), 1)
    return jnp.where(t >= s, jnp.exp(wide - row), 0.0)


def remote(src, dst, send, recv, axis, target):
    return pltpu.make_async_remote_copy(
        src_ref=src, dst_ref=dst, send_sem=send, recv_sem=recv,
        device_id={axis: target}, device_id_type=MESH,
    )


def loop(count, body):
    lax.fori_loop(0, count, lambda i, c: (body(i), c)[1], 0)


class Chain:
    def __init__(self, n, reverse, bufs):
        (self.lsend, self.lrecv, self.zsend, self.zrecv, self.xsend, self.xrecv, self.sems) = bufs
        me = lax.axis_index("seq")
        self.partner = me + 1 - 2 * lax.rem(me, 2)
        place = n - 1 - me if reverse else me
        self.later = lax.rem(place, 2)
        self.row = place // 2
        self.first = self.row == 0
        self.last = self.row == n // 2 - 1
        step = -2 if reverse else 2
        self.next = lax.rem(me + step + n, n)

    def leads(self, h):
        return lax.rem(h, 2) != self.later

    def copy_l(self, h):
        return remote(self.lsend.at[h], self.lrecv.at[h], self.sems.at[0, h], self.sems.at[1, h], "seq", self.partner)

    def copy_x(self, h):
        return remote(self.xsend.at[h], self.xrecv.at[h], self.sems.at[2, h], self.sems.at[3, h], "seq", self.partner)

    def copy_z(self, h):
        return remote(self.zsend.at[h], self.zrecv.at[h], self.sems.at[4, h], self.sems.at[5, h], "seq", self.next)

    def start(self):
        @pl.when(self.first)
        def _():
            self.zrecv[...] = jnp.zeros_like(self.zrecv)

    def give(self, h, state, decay):
        self.lsend[h, 0:DH] = state
        self.lsend[h, DH : DH + 8] = jnp.broadcast_to(decay, (8, DH))

        @pl.when(jnp.logical_not(self.leads(h)))
        def _():
            self.copy_l(h).start()

    def step(self, h, state_in):
        @pl.when(self.leads(h))
        def _():
            self.copy_l(h).wait_recv()

            @pl.when(jnp.logical_not(self.first))
            def _():
                self.copy_z(h).wait_recv()

            state = self.zrecv[h]

            @pl.when(self.later == 1)
            def _():
                mid = self.lrecv[h, DH : DH + 1] * state + self.lrecv[h, 0:DH]
                self.xsend[h] = state
                self.copy_x(h).start()
                self.zsend[h] = self.lsend[h, DH : DH + 1] * mid + self.lsend[h, 0:DH]
                state_in[h] = mid

            @pl.when(self.later == 0)
            def _():
                mid = self.lsend[h, DH : DH + 1] * state + self.lsend[h, 0:DH]
                self.xsend[h] = mid
                self.copy_x(h).start()
                self.zsend[h] = self.lrecv[h, DH : DH + 1] * mid + self.lrecv[h, 0:DH]
                state_in[h] = state

            @pl.when(jnp.logical_not(self.last))
            def _():
                self.copy_z(h).start()

    def take(self, h, state_in):
        @pl.when(jnp.logical_not(self.leads(h)))
        def _():
            self.copy_x(h).wait_recv()
            state_in[h] = self.xrecv[h]

    def finish(self, h):
        @pl.when(self.leads(h))
        def _():
            self.copy_x(h).wait_send()

            @pl.when(jnp.logical_not(self.last))
            def _():
                self.copy_z(h).wait_send()

        @pl.when(jnp.logical_not(self.leads(h)))
        def _():
            self.copy_l(h).wait_send()


def main_kernel(
    n, peers, chunk,
    q_hbm, k_hbm, v_hbm, g_hbm, ld_ref, gain_ref,
    q, k, v, g, att, obuf, r_out, cum_ref, gg_out,
    s_out, lc, state_in, sq_acc, in_acc,
    stat_send, stat_recv, gain_send, gain_recv, inv_b, cen_b,
    lsend1, lrecv1, zsend1, zrecv1, xsend1, xrecv1,
    lsend2, lrecv2, zsend2, zrecv2, xsend2, xrecv2,
    load_sem, chain1_sem, chain2_sem, stat_sem, gain_sem,
):
    heads, tokens, _ = q.shape
    chunks = tokens // chunk
    me = lax.axis_index("seq")
    my_head = lax.axis_index("head")
    columns = heads * DH * peers

    def load(i, hbm, vmem, h):
        where = pl.ds(pl.multiple_of(h * DH, DH), DH)
        return pltpu.make_async_copy(hbm.at[:, where], vmem.at[h], load_sem.at[i, h])

    def load_kv(h):
        load(0, k_hbm, k, h).start()
        load(1, v_hbm, v, h).start()

    def load_q(h):
        load(2, q_hbm, q, h).start()

    def load_g(h):
        load(3, g_hbm, g, h).start()

    loop(heads, load_kv)
    loop(heads, load_q)
    loop(heads, load_g)

    barrier = pltpu.get_barrier_semaphore()
    for off in range(1, n):
        pl.semaphore_signal(barrier, inc=1, device_id={"seq": lax.rem(me + off, n)}, device_id_type=MESH)
    for off in range(1, peers):
        pl.semaphore_signal(barrier, inc=1, device_id={"head": lax.rem(my_head + off, peers)}, device_id_type=MESH)
    chunk_cumsum(ld_ref, cum_ref, chunk)
    forward = Chain(n, False, (lsend1, lrecv1, zsend1, zrecv1, xsend1, xrecv1, chain1_sem))
    backward = Chain(n, True, (lsend2, lrecv2, zsend2, zrecv2, xsend2, xrecv2, chain2_sem))
    forward.start()
    backward.start()
    pl.semaphore_wait(barrier, n - 1 + peers - 1)

    def local_state(h):
        load(0, k_hbm, k, h).wait()
        load(1, v_hbm, v, h).wait()
        state = None
        for j in range(chunks):
            span = slice(j * chunk, (j + 1) * chunk)
            _, column = cum_forms(cum_ref, h, j, chunk)
            total = column[chunk - 1 : chunk, :]
            tail = jnp.exp(total - column)
            part = mm((k[h, span].astype(F32) * tail).astype(BF16), v[h, span], ATB)
            lc[h, j] = part
            state = part if j == 0 else jnp.exp(total) * state + part
            decay = total if j == 0 else decay + total
        forward.give(h, state, jnp.exp(decay))

    loop(heads, local_state)

    def intra(h):
        load(2, q_hbm, q, h).wait()
        for j in range(chunks):
            span = slice(j * chunk, (j + 1) * chunk)
            row, column = cum_forms(cum_ref, h, j, chunk)
            scores = mm(q[h, span], k[h, span], ABT)
            weights = (scores * decay_of(row, column)).astype(BF16)
            att[h, span] = mm(weights, v[h, span], AB)

    sq_acc[...] = jnp.zeros_like(sq_acc)
    in_acc[...] = jnp.zeros_like(in_acc)

    def inter(h):
        load(3, g_hbm, g, h).wait()
        forward.take(h, state_in)
        state = state_in[h]
        gain = gain_ref[pl.ds(h, 1), :]
        for j in range(chunks):
            span = slice(j * chunk, (j + 1) * chunk)
            _, column = cum_forms(cum_ref, h, j, chunk)
            rounded = state.astype(BF16)
            s_out[h, j] = rounded
            whole = att[h, span] + jnp.exp(column) * mm(q[h, span], rounded, AB)
            att[h, span] = whole
            sq_acc[span] += whole * whole
            in_acc[span] += g[h, span].astype(F32) * gain * whole
            if j < chunks - 1:
                state = jnp.exp(column[chunk - 1 : chunk, :]) * state + lc[h, j]

    lag = forward.row * 2 + 1

    def overlap(i):
        @pl.when(i < heads)
        def _():
            intra(i)

        at = i - lag

        @pl.when(jnp.logical_and(at >= 0, at < heads))
        def _():
            forward.step(at, state_in)

        ready = at - 2

        @pl.when(jnp.logical_and(ready >= 0, ready < heads))
        def _():
            inter(ready)

    loop(heads + n + 2, overlap)

    ones = jnp.ones((8, DH), F32)

    def row_sums(acc):
        return lax.dot_general(ones, acc, (ABT, ((), ())), precision=HIGHEST, preferred_element_type=F32)

    upper = lax.broadcasted_iota(jnp.int32, (8, tokens), 0) < 4
    stat_send[...] = jnp.where(upper, row_sums(sq_acc[...]), row_sums(in_acc[...]))

    def stat_copy(off, slot):
        return remote(stat_send, stat_recv.at[slot], stat_sem.at[0, off], stat_sem.at[1, off], "head", lax.rem(my_head + off, peers))

    for off in range(1, peers):
        stat_copy(off, my_head).start()
    stat_recv[my_head] = stat_send[...]
    for off in range(1, peers):
        stat_copy(off, lax.rem(my_head + peers - off, peers)).wait_recv()
    stats = stat_recv[0]
    for i in range(1, peers):
        stats = stats + stat_recv[i]
    inverse = lax.rsqrt(stats[0:1] / columns + EPSILON)
    center = stats[4:5] * inverse / columns
    inv_b[...] = jnp.broadcast_to(inverse, (DH, tokens)).T
    cen_b[...] = jnp.broadcast_to(center, (DH, tokens)).T

    def normalize(h):
        gain = gain_ref[pl.ds(h, 1), :]
        gain_part = jnp.zeros((1, DH), F32)
        state = None
        for j in reversed(range(chunks)):
            span = slice(j * chunk, (j + 1) * chunk)
            _, column = cum_forms(cum_ref, h, j, chunk)
            normed = att[h, span] * inv_b[span]
            obuf[h, span] = (normed * gain).astype(BF16)
            cotangent = g[h, span].astype(F32)
            gain_part = gain_part + jnp.sum(cotangent * normed, axis=0, keepdims=True)
            grad = (inv_b[span] * (cotangent * gain - normed * cen_b[span])).astype(BF16)
            g[h, span] = grad
            part = mm((q[h, span].astype(F32) * jnp.exp(column)).astype(BF16), grad, ATB)
            lc[h, j] = part
            total = column[chunk - 1 : chunk, :]
            state = part if state is None else jnp.exp(total) * state + part
            decay = total if j == chunks - 1 else decay + total
        backward.give(h, state, jnp.exp(decay))
        gain_send[pl.ds(h, 1), :] = gain_part

    loop(heads, normalize)

    def gain_copy(off, slot):
        return remote(gain_send, gain_recv.at[slot], gain_sem.at[0, off], gain_sem.at[1, off], "seq", lax.rem(me + off, n))

    for off in range(1, n):
        gain_copy(off, me).start()
    gain_recv[me] = gain_send[...]

    def gradients(h):
        for j in range(chunks):
            span = slice(j * chunk, (j + 1) * chunk)
            row, column = cum_forms(cum_ref, h, j, chunk)
            decay = decay_of(row, column)
            queries, keys, values, grad = q[h, span], k[h, span], v[h, span], g[h, span]
            weights = (mm(queries, keys, ABT) * decay).astype(BF16)
            grad_weights = (mm(grad, values, ABT) * decay).astype(BF16)
            q[h, span] = (
                mm(grad_weights, keys, AB) + jnp.exp(column) * mm(grad, s_out[h, j], ABT)
            ).astype(BF16)
            att[h, span] = mm(grad_weights, queries, ATB)
            g[h, span] = mm(weights, grad, ATB).astype(BF16)

    back_lag = backward.row * 2 + 1

    def overlap_back(i):
        at = i - back_lag

        @pl.when(jnp.logical_and(at >= 0, at < heads))
        def _():
            backward.step(at, state_in)

        @pl.when(i < heads)
        def _():
            gradients(i)

    loop(heads + n, overlap_back)

    def after(h):
        backward.take(h, state_in)
        state = state_in[h]
        for j in reversed(range(chunks)):
            r_out[h, j] = state.astype(BF16)
            if j > 0:
                _, column = cum_forms(cum_ref, h, j, chunk)
                state = jnp.exp(column[chunk - 1 : chunk, :]) * state + lc[h, j]

    loop(heads, after)

    for off in range(1, n):
        gain_copy(off, lax.rem(me + n - off, n)).wait_recv()
    gain_total = gain_recv[0]
    for i in range(1, n):
        gain_total = gain_total + gain_recv[i]
    gg_out[...] = gain_total

    def finish(h):
        forward.finish(h)
        backward.finish(h)

    loop(heads, finish)
    for off in range(1, peers):
        stat_copy(off, my_head).wait_send()
    for off in range(1, n):
        gain_copy(off, me).wait_send()


def last_kernel(
    chunk, k, v, gq, gk, gv, out, after, cum_ref,
    out_hbm, gq_hbm, gk_hbm, gv_hbm, k_stage, v_stage, store_sem,
):
    heads, tokens, _ = k.shape

    def store(i, vmem, hbm, h):
        where = pl.ds(pl.multiple_of(h * DH, DH), DH)
        return pltpu.make_async_copy(vmem.at[h], hbm.at[:, where], store_sem.at[i, h])

    def copies(h):
        return (
            store(0, out, out_hbm, h), store(1, gq, gq_hbm, h),
            store(2, k_stage, gk_hbm, h), store(3, v_stage, gv_hbm, h),
        )

    def one(h):
        ready = copies(h)
        ready[0].start()
        ready[1].start()
        for j in range(tokens // chunk):
            span = slice(j * chunk, (j + 1) * chunk)
            _, column = cum_forms(cum_ref, h, j, chunk)
            tail = jnp.exp(column[chunk - 1 : chunk, :] - column)
            k_stage[h, span] = (gk[h, span] + tail * mm(v[h, span], after[h, j], ABT)).astype(BF16)
            v_stage[h, span] = (
                gv[h, span].astype(F32) + tail * mm(k[h, span], after[h, j], AB)
            ).astype(BF16)
        ready[2].start()
        ready[3].start()

    def wait(h):
        for copy in copies(h):
            copy.wait()

    loop(heads, one)
    loop(heads, wait)


def on_device(n, peers, queries, key_rows, value_rows, log_decay, norm_gain, grad_out):
    tokens, width = queries.shape
    heads = width // DH
    chunk = CHUNK if tokens % CHUNK == 0 else tokens
    chunks = tokens // chunk
    gain = norm_gain.reshape(heads, DH)
    anywhere = pl.BlockSpec(memory_space=pl.ANY)
    vmem = pl.BlockSpec(memory_space=pltpu.VMEM)
    rows = jax.ShapeDtypeStruct((tokens, width), BF16)
    states = jax.ShapeDtypeStruct((heads, chunks, DH, DH), BF16)
    per_head = lambda *shape, dtype=F32: pltpu.VMEM((heads, *shape), dtype)
    chain = [
        per_head(DH + 8, DH), per_head(DH + 8, DH), per_head(DH, DH),
        per_head(DH, DH), per_head(DH, DH), per_head(DH, DH),
    ]
    dma = pltpu.SemaphoreType.DMA
    by_head = lambda dtype: pltpu.VMEM((heads, tokens, DH), dtype)
    *held, grad_gain = pl.pallas_call(
        functools.partial(main_kernel, n, peers, chunk),
        out_shape=(
            by_head(BF16), by_head(BF16), by_head(BF16), by_head(BF16), by_head(F32), by_head(BF16),
            pltpu.VMEM((heads, chunks, DH, DH), BF16), pltpu.VMEM((heads, tokens), F32),
            jax.ShapeDtypeStruct((heads, DH), F32),
        ),
        in_specs=[anywhere] * 4 + [vmem] * 2,
        out_specs=(vmem,) * 9,
        scratch_shapes=[
            per_head(chunks, DH, DH, dtype=BF16), per_head(chunks, DH, DH), per_head(DH, DH),
            pltpu.VMEM((tokens, DH), F32), pltpu.VMEM((tokens, DH), F32),
            pltpu.VMEM((8, tokens), F32), pltpu.VMEM((peers, 8, tokens), F32),
            pltpu.VMEM((heads, DH), F32), pltpu.VMEM((n, heads, DH), F32),
            pltpu.VMEM((tokens, DH), F32), pltpu.VMEM((tokens, DH), F32),
            *chain, *chain,
            dma((4, heads)), dma((6, heads)), dma((6, heads)),
            dma((2, peers)), dma((2, n)),
        ],
        compiler_params=pltpu.CompilerParams(
            collective_id=0, has_side_effects=True, vmem_limit_bytes=32 * 1024 * 1024
        ),
        name="forward_chain",
    )(queries, key_rows, value_rows, grad_out, log_decay, gain)
    grad_q, key_held, value_held, grad_v, grad_k, out, after, cumulative = held
    out, grad_q, grad_k, grad_v = pl.pallas_call(
        functools.partial(last_kernel, chunk),
        out_shape=(rows,) * 4,
        in_specs=[vmem] * 8,
        out_specs=(anywhere,) * 4,
        scratch_shapes=[
            per_head(tokens, DH, dtype=BF16), per_head(tokens, DH, dtype=BF16), dma((4, heads)),
        ],
        compiler_params=pltpu.CompilerParams(vmem_limit_bytes=16 * 1024 * 1024),
        name="last_terms",
    )(key_held, value_held, grad_q, grad_k, grad_v, out, after, cumulative)
    return out, grad_q, grad_k, grad_v, grad_gain.reshape(width)


def solution(mesh):
    in_specs = (
        P("seq", "head"),
        P("seq", "head"),
        P("seq", "head"),
        P("head", "seq"),
        P("head"),
        P("seq", "head"),
    )
    out_specs = (P("seq", "head"), P("seq", "head"), P("seq", "head"), P("seq", "head"), P("head"))
    return jax.shard_map(
        functools.partial(on_device, mesh.shape["seq"], mesh.shape["head"]),
        mesh=mesh, in_specs=in_specs, out_specs=out_specs, check_vma=False,
    )
```
